32 devices in a mesh: row: 8 (over y, x, core), col: 4 (over z).
Axes of the slice: x: 2, y: 2, z: 4, core: 2. Of those that a mesh axis runs over, the one named last changes fastest.
Arguments:
- eigvecs: float32 [2048, 4096], P('row', 'col'), may hold values from -6 to 6
- reflectors: float32 [8, 8, 64, 192], P('row'), may hold values from -0.5 to 1.5, as said below
- factors: float32 [8, 8, 64, 64], P('row'), may hold values from -3 to 3, as said below
- first_block: int32 [8], replicated, may hold values from 0 to 7
- live_count: int32 [4], P('col'), may hold values from 128 to 768
Outputs:
- vectors: float32 [2048, 4096], P('row', 'col')
The draws below stay inside these ranges and needn't reach their ends.
Inputs may be any that keep to these rules, and one draw needn't show every extreme that they name: reflectors[w, g, j, 0] lies in 1 to 1.5; the other entries are small. factors[w, g] is upper triangular, and I - V_wg factors[w, g] V_wg^T equals the product over j = 0 .. 63 in order of I - 2 v_j v_j^T / (v_j^T v_j), v_j the columns of V_wg.
All inputs are finite; a program needn't handle non-finite values.
Results may differ from the reference program's by a relative error of at most 0.0003.
Values sent between devices are 32-bit elements; how exact they have to be, the bound alone decides.
No kernel may reach another device: no remote copies, remote signals or barrier semaphores. Data moves between devices by JAX's collectives and lax.ppermute only.
A program may use at most 64 MiB of HBM per device.

```python
import jax
import jax.numpy as jnp
from jax import lax

B = 192
NB = 64
CT = 1024
N = 2048
W = 8
NBT = 8
KC = 4096
N_COL = 4


def expand_draw(compact):
    block_width, band_width = compact.shape[-2:]
    block_rows = block_width + band_width
    padded = jnp.pad(compact, ((0, 0), (0, 0), (0, block_rows + 1 - band_width)))
    flattened = padded.reshape(compact.shape[0], block_width * (block_rows + 1))[:, :block_width * block_rows]
    return jnp.swapaxes(flattened.reshape(compact.shape[0], block_width, block_rows), -1, -2)


def reflector_pair(key):
    base = jax.random.fold_in(key, 7)
    shape = (W, NBT, NB, B)
    values = jnp.clip(0.1 * jax.random.normal(base, shape, jnp.float32), -0.5, 0.5)
    first_entry = jnp.arange(B) == 0
    values = jnp.where(first_entry, jnp.abs(values), values)
    leading = first_entry.astype(jnp.float32)
    compact = values + leading

    def window_factors(window_compact):
        expanded_factor = expand_draw(window_compact)
        gram = jnp.einsum('glr,gls->grs', expanded_factor, expanded_factor, precision=lax.Precision.HIGHEST)
        diagonal = jnp.diagonal(gram, axis1=1, axis2=2)
        upper = jnp.triu(gram, 1) + jax.vmap(jnp.diag)(0.5 * diagonal)
        identity = jnp.broadcast_to(jnp.eye(NB, dtype=jnp.float32), upper.shape)
        return jax.scipy.linalg.solve_triangular(upper, identity, lower=False)
    factors = lax.map(window_factors, compact)
    return (compact, factors)


def draw_reflectors(key, part):
    return reflector_pair(key)[0]


def draw_factors(key, part):
    return reflector_pair(key)[1]


def touch_ends(array, key, low, largest):
    shape = array.shape
    place = [jax.random.randint(jax.random.fold_in(key, axis), (), 0, shape[axis]) for axis in range(len(shape))]
    array = array.at[tuple(place)].set(low)
    longest = shape.index(max(shape))
    place[longest] = (place[longest] + 1) % shape[longest]
    return array.at[tuple(place)].set(largest)


def shard_levels(stream_key, shape, shards, smallest, largest):
    gain, own = 1.0, jax.random.fold_in(stream_key, 6)
    for axis_at, blocks in shards:
        steps = jnp.exp(jax.random.uniform(jax.random.fold_in(own, axis_at), (blocks,), jnp.float32, smallest / len(shards), largest / len(shards)))
        gain = gain * jnp.repeat(steps, shape[axis_at] // blocks).reshape([-1 if axis == axis_at else 1 for axis in range(len(shape))])
    return gain


def centred(key, extent, deviation, most, cuts=(), kind=jnp.bfloat16):
    drawn = jax.random.normal(key, extent, jnp.float32) * deviation
    if len(cuts) > 0:
        drawn = shard_levels(key, extent, cuts, -0.22, 0.18) * drawn
    return jnp.clip(drawn, min=-most, max=most).astype(kind)


def setup_inputs(seed: int = 0) -> dict:
    streams_of = jax.random.split(jax.random.key(seed), 6)
    eigvecs = centred(streams_of[0], (N, KC), 1.0, 6.0, ((0, 8), (1, 4)), jnp.float32)
    reflectors = draw_reflectors(jax.random.fold_in(streams_of[5], 71), 0)
    factors = draw_factors(jax.random.fold_in(streams_of[5], 71), 0)
    first_block = touch_ends(jax.random.randint(streams_of[3], (W,), 0, NBT), jax.random.fold_in(streams_of[3], 1), 0, NBT - 1).astype(jnp.int32)
    live_count = touch_ends(jax.random.randint(streams_of[4], (N_COL,), CT // 8, 3 * CT // 4 + 1), jax.random.fold_in(streams_of[4], 1), CT // 8, (3 * CT // 4 + 1) - 1).astype(jnp.int32)
    return dict(eigvecs=eigvecs, reflectors=reflectors, factors=factors, first_block=first_block, live_count=live_count)


highest_precision = lax.Precision.HIGHEST

def expand(compact):
    leading = compact.shape[:-2]
    block_width, band_width = compact.shape[-2:]
    block_rows = block_width + band_width
    padded = jnp.pad(compact, [(0, 0)] * len(leading) + [(0, 0), (0, block_rows + 1 - band_width)])
    flattened = padded.reshape(leading + (block_width * (block_rows + 1),))[..., :block_width * block_rows]
    return jnp.swapaxes(flattened.reshape(leading + (block_width, block_rows)), -1, -2)

def apply_blocks(eigenvector_blocks, compact, factor):
    expanded_factor = expand(compact)
    correlation_matrix = jnp.einsum('kpx,kpi->kxi', expanded_factor, eigenvector_blocks, precision=highest_precision)
    correlation_matrix = jnp.einsum('grs,gsc->grc', factor, correlation_matrix, precision=highest_precision)
    return eigenvector_blocks - jnp.einsum('nfu,nuo->nfo', expanded_factor, correlation_matrix, precision=highest_precision)

def reference(eigvecs, reflectors, factors, first_block, live_count):
    block_rows = NB + B
    half_block = block_rows // 2
    vectors = eigvecs
    block_index = jnp.arange(NBT, dtype=jnp.int32)
    for window in range(W):
        active_window = (block_index >= first_block[window])[:, None, None]
        if window % 2 == 0:
            blocks = vectors.reshape(NBT, block_rows, KC)
            updated = apply_blocks(blocks, reflectors[window], factors[window])
            vectors = jnp.where(active_window, updated, blocks).reshape(N, KC)
        else:
            blocks = vectors[half_block:N - half_block].reshape(NBT - 1, block_rows, KC)
            updated = apply_blocks(blocks, reflectors[window, :NBT - 1], factors[window, :NBT - 1])
            updated = jnp.where(active_window[:NBT - 1], updated, blocks).reshape(N - block_rows, KC)
            vectors = jnp.concatenate([vectors[:half_block], updated, vectors[N - half_block:]], axis=0)
    slot_index = jnp.arange(KC, dtype=jnp.int32) % CT
    column_group = jnp.arange(KC, dtype=jnp.int32) // CT
    kept_mask = slot_index < live_count[column_group]
    return jnp.where(kept_mask[None, :], vectors, jnp.zeros_like(vectors))
```

```python
import functools

import jax
import jax.numpy as jnp
from jax import lax
from jax.experimental import pallas as pl
from jax.experimental.pallas import tpu as pltpu
from jax.sharding import PartitionSpec as P

VMEM = pl.BlockSpec(memory_space=pltpu.VMEM)
SMEM = pl.BlockSpec(memory_space=pltpu.SMEM)
NN = (((1,), (0,)), ((), ()))
NT = (((1,), (1,)), ((), ()))
TN = (((0,), (0,)), ((), ()))
EXTRA_ROWS = 8


def split(x):
    high = x.astype(jnp.bfloat16)
    return high, (x - high.astype(jnp.float32)).astype(jnp.bfloat16)


def product(left, right, dims=NN):
    dot = functools.partial(
        lax.dot_general, dimension_numbers=dims, preferred_element_type=jnp.float32
    )
    return dot(left[0], right[0]) + (dot(left[0], right[1]) + dot(left[1], right[0]))


def square_iota(shape):
    return lax.broadcasted_iota(jnp.int32, shape, 0), lax.broadcasted_iota(jnp.int32, shape, 1)


def pack_kernel(position_ref, compact_ref, factor_ref, packed_ref):
    _, blocks, width, band = compact_ref.shape
    half = (width + band) // 2
    odd = position_ref[0] % 2 == 1
    row, column = square_iota((width, band))
    upper_part = row + column < half
    frow, fcolumn = square_iota((width, width))

    @pl.when(jnp.logical_not(odd))
    def _():
        for block in range(blocks):
            packed_ref[block, :width, :band] = compact_ref[0, block]
            packed_ref[block, :width, band:] = factor_ref[0, block]
            packed_ref[block, width:, :] = jnp.zeros_like(packed_ref[block, width:, :])

    @pl.when(odd)
    def _():
        for block in range(blocks):
            before = max(block - 1, 0)
            packed_ref[block, :width, :band] = jnp.where(
                upper_part, compact_ref[0, block], compact_ref[0, before]
            )
            other = factor_ref[0, before]
            packed_ref[block, :width, band:] = jnp.where(
                frow <= fcolumn, factor_ref[0, block], other.T
            )
            diagonal = jnp.sum(jnp.where(frow == fcolumn, other, 0.0), axis=0, keepdims=True)
            packed_ref[block, width:, :] = jnp.zeros_like(packed_ref[block, width:, :])
            packed_ref[block, width:, band:] = jnp.broadcast_to(diagonal, (EXTRA_ROWS, width))


def skew(packed, band):
    _, column = square_iota(packed.shape)
    return pltpu.roll(jnp.where(column < band, packed, 0.0), 0, 1, stride=1, stride_axis=0)


def read_even(packed_ref, window, width, position, first_ref):
    total = packed_ref.shape[-1]
    band = total - width
    packed = packed_ref[window, :width, :]
    transposed = split(skew(packed, band))
    active = (position >= first_ref[window]).astype(jnp.float32)
    factor = split(packed[:, band:] * active)
    return transposed, split(product(factor, transposed))


def read_odd(packed_ref, window, width, position, count, first_ref):
    total = packed_ref.shape[-1]
    band = total - width
    half = total // 2
    packed = packed_ref[window, :width, :]
    skewed = skew(packed, band)
    nothing = jnp.zeros((width, half), jnp.float32)
    above = jnp.concatenate([skewed[:, half:], nothing], axis=1)
    below = jnp.concatenate([nothing, skewed[:, :half]], axis=1)
    mixed = packed[:, band:]
    diagonal = packed_ref[window, width : width + EXTRA_ROWS, band:][:1]
    row, column = square_iota((width, width))
    first = first_ref[window]
    above_on = ((position >= 1) & (position - 1 >= first)).astype(jnp.float32)
    below_on = ((position < count - 1) & (position >= first)).astype(jnp.float32)
    factor_below = jnp.where(row <= column, mixed, 0.0) * below_on
    factor_above = jnp.where(row < column, mixed.T, jnp.where(row == column, diagonal, 0.0)) * above_on
    odd = position % 2 == 1
    rows = jnp.concatenate([jnp.where(odd, below, above), jnp.where(odd, above, below)], axis=0)
    square = jnp.zeros((width, width), jnp.float32)
    factor = jnp.concatenate(
        [
            jnp.concatenate([jnp.where(odd, factor_below, factor_above), square], axis=1),
            jnp.concatenate([square, jnp.where(odd, factor_above, factor_below)], axis=1),
        ],
        axis=0,
    )
    return rows, split(factor)


def split_kernel(z_ref, high_ref, low_ref):
    high_ref[...], low_ref[...] = split(z_ref[...])


def first_kernel(count, width, position_ref, first_ref, packed_ref, high_ref, low_ref, cross_ref, own_ref):
    position = position_ref[0]
    transposed, scaled = read_even(packed_ref, 0, width, position, first_ref)
    rows, _ = read_odd(packed_ref, 1, width, position, count, first_ref)
    through = rows - product(split(product(split(rows), transposed, NT)), scaled)
    partial = product(split(through), (high_ref[...], low_ref[...]))
    cross_ref[...] = partial[:width]
    own_ref[...] = partial[width:]


def ahead_kernel(
    count, width, window, start, last, position_ref, first_ref, packed_ref, order_ref, *refs
):
    position = position_ref[0]
    if start:
        high_ref, low_ref, *out = refs
        transposed, scaled = read_even(packed_ref, 0, width, position, first_ref)
        z_split = (high_ref[...], low_ref[...])
        z = high_ref[...].astype(jnp.float32) + low_ref[...].astype(jnp.float32)
        z = z - product(transposed, split(product(scaled, z_split)), TN)
    else:
        z_ref, update_high, update_low, sum_high, sum_low, *out = refs
        z = z_ref[...] - product(
            (update_high[...], update_low[...]), (sum_high[...], sum_low[...])
        )
    rows, factor = read_odd(packed_ref, window, width, position, count, first_ref)
    update = product(split(rows), factor, TN)
    if last:
        out[0][...] = z
        out[1][...], out[2][...] = split(update)
        return
    z_out, base_out, update_high, update_low, mix_high, mix_low = out
    z_split = split(z)
    transposed, scaled = read_even(packed_ref, window + 1, width, position, first_ref)
    next_rows, _ = read_odd(packed_ref, window + 2, width, position, count, first_ref)
    through = next_rows - product(split(product(split(next_rows), transposed, NT)), scaled)
    through = split(through)
    update_split = split(update)
    mix_high[...], mix_low[...] = split(product(through, update_split))
    base_out[...] = product(through, z_split)
    moved = update - product(transposed, split(product(scaled, update_split)), TN)
    update_high[...], update_low[...] = split(moved)
    z_out[...] = z - product(transposed, split(product(scaled, z_split)), TN)


def step_kernel(
    width, cross, own, cross_in, own_in, base, mix_high, mix_low, cross_out, own_out, sum_high, sum_low
):
    total = jnp.concatenate([cross[...] + cross_in[...], own[...] + own_in[...]], axis=0)
    total = split(total)
    sum_high[...], sum_low[...] = total
    partial = base[...] - product((mix_high[...], mix_low[...]), total)
    cross_out[...] = partial[:width]
    own_out[...] = partial[width:]


def last_kernel(live_ref, cross, own, cross_in, own_in, z_ref, update_high, update_low, out_ref):
    total = jnp.concatenate([cross[...] + cross_in[...], own[...] + own_in[...]], axis=0)
    z = z_ref[...] - product((update_high[...], update_low[...]), split(total))
    kept = z.shape[1]
    _, column = square_iota(z.shape)
    out_ref[:, :kept] = jnp.where(column < live_ref[0], z, 0.0)
    out_ref[:, kept:] = jnp.zeros((z.shape[0], out_ref.shape[1] - kept), jnp.float32)


def call(kernel, outs, ins, *operands, flops=0):
    shapes = [jax.ShapeDtypeStruct(shape, dtype) for shape, dtype in outs]
    return pl.pallas_call(
        kernel,
        out_shape=shapes,
        in_specs=ins,
        out_specs=[VMEM] * len(shapes),
        cost_estimate=pl.CostEstimate(flops=flops, bytes_accessed=1 << 20, transcendentals=0),
        compiler_params=pltpu.CompilerParams(vmem_limit_bytes=40 << 20),
    )(*operands)


def body(eigvecs, reflectors, factors, first_block, live_count):
    count = lax.axis_size("row")
    position = lax.axis_index("row").astype(jnp.int32).reshape(1)
    row_count, col_count = eigvecs.shape
    share, blocks, width, band = reflectors.shape
    block_rows = width + band
    assert row_count == block_rows and share == 1 and blocks == count
    windows = share * count
    kept = 3 * col_count // 4
    f32, bf16 = jnp.float32, jnp.bfloat16

    packed = call(
        pack_kernel,
        [((blocks, width + EXTRA_ROWS, block_rows), f32)],
        [SMEM, VMEM, VMEM],
        position,
        reflectors,
        factors,
    )[0]
    packed = lax.all_to_all(packed, "row", split_axis=0, concat_axis=0, tiled=True)
    high, low = pl.pallas_call(
        split_kernel,
        grid=(1,),
        out_shape=[jax.ShapeDtypeStruct((row_count, kept), bf16)] * 2,
        in_specs=[pl.BlockSpec((row_count, kept), lambda i: (0, 0))],
        out_specs=[pl.BlockSpec((row_count, kept), lambda i: (0, 0))] * 2,
    )(eigvecs)

    def swap(x, start):
        pairs = [(i, i + 1) for i in range(start, count - 1, 2)]
        return lax.ppermute(x, "row", pairs + [(j, i) for i, j in pairs])

    small = ((width, kept), f32)
    double = ((2 * width, kept), bf16)
    cross, own = call(
        functools.partial(first_kernel, count, width),
        [small, small],
        [SMEM, SMEM] + [VMEM] * 3,
        position,
        first_block,
        packed,
        high,
        low,
    )
    state = (high, low)
    for window in range(1, windows, 2):
        last = window == windows - 1
        cross_in, own_in = swap(cross, 1), swap(own, 0)
        update = ((row_count, 2 * width), bf16)
        mix = ((2 * width, 2 * width), bf16)
        outs = [((row_count, kept), f32)]
        outs += [update, update] if last else [((2 * width, kept), f32), update, update, mix, mix]
        ahead = call(
            functools.partial(ahead_kernel, count, width, window, window == 1, last),
            outs,
            [SMEM, SMEM, VMEM, pl.BlockSpec(memory_space=pl.ANY)] + [VMEM] * len(state),
            position,
            first_block,
            packed,
            cross,
            *state,
            flops=10**9,
        )
        if last:
            z, update_high, update_low = ahead
            return call(
                last_kernel,
                [((row_count, col_count), f32)],
                [SMEM] + [VMEM] * 7,
                live_count,
                cross,
                own,
                cross_in,
                own_in,
                z,
                update_high,
                update_low,
            )[0]
        z, base, update_high, update_low, mix_high, mix_low = ahead
        cross, own, sum_high, sum_low = call(
            functools.partial(step_kernel, width),
            [small, small, double, double],
            [VMEM] * 7,
            cross,
            own,
            cross_in,
            own_in,
            base,
            mix_high,
            mix_low,
        )
        state = (z, update_high, update_low, sum_high, sum_low)


def solution(mesh):
    placed = (
        P("row", "col"),
        P("row", None, None, None),
        P("row", None, None, None),
        P(),
        P("col"),
    )
    return jax.shard_map(
        body, mesh=mesh, in_specs=placed, out_specs=P("row", "col"), check_vma=False
    )
```

```python
import functools

import jax
import jax.numpy as jnp
from jax import lax
from jax.experimental import pallas as pl
from jax.experimental.pallas import tpu as pltpu
from jax.sharding import PartitionSpec as P

VMEM = pl.BlockSpec(memory_space=pltpu.VMEM)
SMEM = pl.BlockSpec(memory_space=pltpu.SMEM)
NN = (((1,), (0,)), ((), ()))
NT = (((1,), (1,)), ((), ()))
TN = (((0,), (0,)), ((), ()))
ANY = pl.BlockSpec(memory_space=pl.ANY)
HBM = pl.BlockSpec(memory_space=pltpu.HBM)
PIECES = 3


def split(x):
    high = x.astype(jnp.bfloat16)
    return high, (x - high.astype(jnp.float32)).astype(jnp.bfloat16)


def product(left, right, dims=NN):
    dot = functools.partial(
        lax.dot_general, dimension_numbers=dims, preferred_element_type=jnp.float32
    )
    return dot(left[0], right[0]) + (dot(left[0], right[1]) + dot(left[1], right[0]))


def square_iota(shape):
    return lax.broadcasted_iota(jnp.int32, shape, 0), lax.broadcasted_iota(jnp.int32, shape, 1)


def pack_kernel(position_ref, compact_hbm, factor_hbm, packed_hbm, compact_ref, factor_ref, packed_ref, in_sems, out_sems):
    blocks, width, band = compact_ref.shape
    half = (width + band) // 2
    row, column = square_iota((width, band))
    upper_part = row + column < half
    frow, fcolumn = square_iota((width, width))

    def fetch(block):
        return (
            pltpu.make_async_copy(compact_hbm.at[0, block], compact_ref.at[block], in_sems.at[0, block]),
            pltpu.make_async_copy(factor_hbm.at[0, block], factor_ref.at[block], in_sems.at[1, block]),
        )

    def deliver(block):
        return pltpu.make_async_copy(packed_ref.at[block], packed_hbm.at[block], out_sems.at[block])

    def scaled(block):
        factor = factor_ref[block]
        diagonal = jnp.where(frow == fcolumn, factor, 0.0)
        down = jnp.sqrt(jnp.sum(diagonal, axis=1, keepdims=True) * 0.5)
        across = jnp.sqrt(jnp.sum(diagonal, axis=0, keepdims=True) * 0.5)
        return compact_ref[block] * down, factor / (down * across)

    for block in range(blocks):
        for copy in fetch(block):
            copy.start()

    @pl.when(position_ref[0] % 2 == 0)
    def _():
        for block in range(blocks):
            for copy in fetch(block):
                copy.wait()
            packed_ref[block, :, :band] = compact_ref[block]
            packed_ref[block, :, band:] = factor_ref[block]
            deliver(block).start()

    @pl.when(position_ref[0] % 2 == 1)
    def _():
        before = None
        for block in range(blocks):
            for copy in fetch(block):
                copy.wait()
            compact, factor = scaled(block)
            other_compact, other_factor = before or (compact, factor)
            packed_ref[block, :, :band] = jnp.where(upper_part, compact, other_compact)
            packed_ref[block, :, band:] = jnp.where(frow <= fcolumn, factor, other_factor.T)
            deliver(block).start()
            before = compact, factor

    for block in range(blocks):
        deliver(block).wait()


def skew(packed, band):
    _, column = square_iota(packed.shape)
    return pltpu.roll(jnp.where(column < band, packed, 0.0), 0, 1, stride=1, stride_axis=0)


def read_even(packed_ref, flags_ref, window, width):
    band = packed_ref.shape[-1] - width
    packed = packed_ref[window]
    transposed = split(skew(packed, band))
    factor = split(packed[:, band:] * flags_ref[window, :1, :1])
    return transposed, split(product(factor, transposed))


def read_odd(packed_ref, flags_ref, window, width):
    total = packed_ref.shape[-1]
    band = total - width
    half = total // 2
    packed = packed_ref[window]
    skewed = skew(packed, band)
    nothing = jnp.zeros((width, half), jnp.float32)
    above = jnp.concatenate([skewed[:, half:], nothing], axis=1)
    below = jnp.concatenate([nothing, skewed[:, :half]], axis=1)
    mixed = packed[:, band:]
    row, column = square_iota((width, width))
    diagonal = jnp.where(row == column, 2.0, 0.0)
    factor_below = jnp.where(row < column, mixed, diagonal) * flags_ref[window, 0:1, :1]
    factor_above = jnp.where(row < column, mixed.T, diagonal) * flags_ref[window, 1:2, :1]
    odd = flags_ref[window, 2:3, :1] > 0.5
    rows = jnp.concatenate([jnp.where(odd, below, above), jnp.where(odd, above, below)], axis=0)
    square = jnp.zeros((width, width), jnp.float32)
    factor = jnp.concatenate(
        [
            jnp.concatenate([jnp.where(odd, factor_below, factor_above), square], axis=1),
            jnp.concatenate([square, jnp.where(odd, factor_above, factor_below)], axis=1),
        ],
        axis=0,
    )
    return rows, split(factor)


def split_kernel(count, position_ref, first_ref, z_hbm, high_ref, low_ref, flags_ref, z_ref, sem):
    copy = pltpu.make_async_copy(z_hbm.at[:, : z_ref.shape[1]], z_ref, sem)
    copy.start()
    position = position_ref[0]
    row, _ = square_iota(flags_ref.shape[1:])
    for window in range(flags_ref.shape[0]):
        first = first_ref[window]
        if window % 2 == 0:
            flags = jnp.where(position >= first, 1.0, 0.0)
            flags_ref[window] = jnp.full(flags_ref.shape[1:], flags, jnp.float32)
        else:
            below = jnp.where((position < count - 1) & (position >= first), 1.0, 0.0)
            above = jnp.where((position >= 1) & (position - 1 >= first), 1.0, 0.0)
            odd = jnp.where(position % 2 == 1, 1.0, 0.0)
            flags_ref[window] = jnp.where(row == 0, below, jnp.where(row == 1, above, odd))
    copy.wait()
    high_ref[...], low_ref[...] = split(z_ref[...])


def first_kernel(width, flags_ref, packed_ref, high_ref, low_ref, cross_ref, own_ref):
    transposed, scaled = read_even(packed_ref, flags_ref, 0, width)
    rows, _ = read_odd(packed_ref, flags_ref, 1, width)
    through = rows - product(split(product(split(rows), transposed, NT)), scaled)
    partial = product(split(through), (high_ref[...], low_ref[...]))
    cross_ref[...] = partial[:width]
    own_ref[...] = partial[width:]


def ahead_kernel(width, window, start, last, flags_ref, packed_ref, order_ref, *refs):
    if start:
        high_ref, low_ref, *out = refs
        transposed, scaled = read_even(packed_ref, flags_ref, 0, width)
        z_split = (high_ref[...], low_ref[...])
        z = high_ref[...].astype(jnp.float32) + low_ref[...].astype(jnp.float32)
        z = z - product(transposed, split(product(scaled, z_split)), TN)
    else:
        z_ref, update_high, update_low, sum_high, sum_low, *out = refs
        z = z_ref[...] - product(
            (update_high[...], update_low[...]), (sum_high[...], sum_low[...])
        )
    rows, factor = read_odd(packed_ref, flags_ref, window, width)
    update = product(split(rows), factor, TN)
    if last:
        out[0][...] = z
        out[1][...], out[2][...] = split(update)
        return
    z_out, base_out, update_high, update_low, mix_high, mix_low = out
    z_split = split(z)
    transposed, scaled = read_even(packed_ref, flags_ref, window + 1, width)
    next_rows, _ = read_odd(packed_ref, flags_ref, window + 2, width)
    through = next_rows - product(split(product(split(next_rows), transposed, NT)), scaled)
    through = split(through)
    update_split = split(update)
    mix_high[...], mix_low[...] = split(product(through, update_split))
    base_out[...] = product(through, z_split)
    moved = update - product(transposed, split(product(scaled, update_split)), TN)
    update_high[...], update_low[...] = split(moved)
    z_out[...] = z - product(transposed, split(product(scaled, z_split)), TN)


def step_kernel(
    width, cross, own, cross_in, own_in, base, mix_high, mix_low, cross_out, own_out, sum_high, sum_low
):
    total = jnp.concatenate([cross[...] + cross_in[...], own[...] + own_in[...]], axis=0)
    total = split(total)
    sum_high[...], sum_low[...] = total
    partial = base[...] - product((mix_high[...], mix_low[...]), total)
    cross_out[...] = partial[:width]
    own_out[...] = partial[width:]


def last_kernel(live_ref, cross, own, cross_in, own_in, z_ref, update_high, update_low, out_hbm, out_ref, sems):
    rows, kept = z_ref.shape
    total = out_ref.shape[1]
    pieces = PIECES
    size = kept // pieces

    def deliver(piece):
        begin, end = piece * size, (piece + 1) * size if piece < pieces else total
        return pltpu.make_async_copy(
            out_ref.at[:, begin:end], out_hbm.at[:, begin:end], sems.at[piece]
        )

    out_ref[:, kept:] = jnp.zeros((rows, total - kept), jnp.float32)
    deliver(pieces).start()
    for piece in range(pieces):
        here = slice(piece * size, (piece + 1) * size)
        sums = jnp.concatenate([cross[:, here] + cross_in[:, here], own[:, here] + own_in[:, here]], axis=0)
        z = z_ref[:, here] - product((update_high[...], update_low[...]), split(sums))
        _, column = square_iota(z.shape)
        out_ref[:, here] = jnp.where(column + piece * size < live_ref[0], z, 0.0)
        deliver(piece).start()
    for piece in range(pieces + 1):
        deliver(piece).wait()


def call(kernel, outs, ins, *operands, flops=0, scratch=(), out_specs=None, limit=40 << 20):
    shapes = [jax.ShapeDtypeStruct(shape, dtype) for shape, dtype in outs]
    return pl.pallas_call(
        kernel,
        out_shape=shapes,
        in_specs=ins,
        out_specs=out_specs or [VMEM] * len(shapes),
        scratch_shapes=scratch,
        cost_estimate=pl.CostEstimate(flops=flops, bytes_accessed=1 << 20, transcendentals=0),
        compiler_params=pltpu.CompilerParams(vmem_limit_bytes=limit),
    )(*operands)


def body(eigvecs, reflectors, factors, first_block, live_count):
    count = lax.axis_size("row")
    position = lax.axis_index("row").astype(jnp.int32).reshape(1)
    row_count, col_count = eigvecs.shape
    share, blocks, width, band = reflectors.shape
    block_rows = width + band
    assert row_count == block_rows and share == 1 and blocks == count
    windows = share * count
    kept = 3 * col_count // 4
    f32, bf16 = jnp.float32, jnp.bfloat16

    packed = call(
        pack_kernel,
        [((blocks, width, block_rows), f32)],
        [SMEM, HBM, HBM],
        position,
        reflectors,
        factors,
        out_specs=[HBM],
        limit=None,
        scratch=[
            pltpu.VMEM((blocks, width, band), f32),
            pltpu.VMEM((blocks, width, width), f32),
            pltpu.VMEM((blocks, width, block_rows), f32),
            pltpu.SemaphoreType.DMA((2, blocks)),
            pltpu.SemaphoreType.DMA((blocks,)),
        ],
    )[0]
    packed = lax.all_to_all(packed, "row", split_axis=0, concat_axis=0, tiled=True)
    high, low, flags = call(
        functools.partial(split_kernel, count),
        [((row_count, kept), bf16)] * 2 + [((windows, 8, 128), f32)],
        [SMEM, SMEM, HBM],
        position,
        first_block,
        eigvecs,
        scratch=[pltpu.VMEM((row_count, kept), f32), pltpu.SemaphoreType.DMA],
    )

    def swap(x, start):
        pairs = [(i, i + 1) for i in range(start, count - 1, 2)]
        return lax.ppermute(x, "row", pairs + [(j, i) for i, j in pairs])

    small = ((width, kept), f32)
    double = ((2 * width, kept), bf16)
    cross, own = call(
        functools.partial(first_kernel, width),
        [small, small],
        [VMEM] * 4,
        flags,
        packed,
        high,
        low,
    )
    state = (high, low)
    for window in range(1, windows, 2):
        last = window == windows - 1
        cross_in, own_in = swap(cross, 1), swap(own, 0)
        update = ((row_count, 2 * width), bf16)
        mix = ((2 * width, 2 * width), bf16)
        outs = [((row_count, kept), f32)]
        outs += [update, update] if last else [((2 * width, kept), f32), update, update, mix, mix]
        ahead = call(
            functools.partial(ahead_kernel, width, window, window == 1, last),
            outs,
            [VMEM, VMEM, ANY] + [VMEM] * len(state),
            flags,
            packed,
            cross,
            *state,
            flops=10**9,
        )
        if last:
            z, update_high, update_low = ahead
            return call(
                last_kernel,
                [((row_count, col_count), f32)],
                [SMEM] + [VMEM] * 7,
                live_count,
                cross,
                own,
                cross_in,
                own_in,
                z,
                update_high,
                update_low,
                out_specs=[HBM],
                scratch=[pltpu.VMEM((row_count, col_count), f32), pltpu.SemaphoreType.DMA((PIECES + 1,))],
            )[0]
        z, base, update_high, update_low, mix_high, mix_low = ahead
        cross, own, sum_high, sum_low = call(
            functools.partial(step_kernel, width),
            [small, small, double, double],
            [VMEM] * 7,
            cross,
            own,
            cross_in,
            own_in,
            base,
            mix_high,
            mix_low,
        )
        state = (z, update_high, update_low, sum_high, sum_low)


def solution(mesh):
    placed = (
        P("row", "col"),
        P("row", None, None, None),
        P("row", None, None, None),
        P(),
        P("col"),
    )
    return jax.shard_map(
        body, mesh=mesh, in_specs=placed, out_specs=P("row", "col"), check_vma=False
    )
```

```python
import functools

import jax
import jax.numpy as jnp
from jax import lax
from jax.experimental import pallas as pl
from jax.experimental.pallas import tpu as pltpu
from jax.sharding import PartitionSpec as P

VMEM = pl.BlockSpec(memory_space=pltpu.VMEM)
SMEM = pl.BlockSpec(memory_space=pltpu.SMEM)
NN = (((1,), (0,)), ((), ()))
NT = (((1,), (1,)), ((), ()))
TN = (((0,), (0,)), ((), ()))
ANY = pl.BlockSpec(memory_space=pl.ANY)
HBM = pl.BlockSpec(memory_space=pltpu.HBM)
PIECES = 3
DEPTH = 256
TAIL = 8


def split(x):
    high = x.astype(jnp.bfloat16)
    return high, (x - high.astype(jnp.float32)).astype(jnp.bfloat16)


def product(left, right, dims=NN):
    ((left_axis,), (right_axis,)), _ = dims
    depth = left[0].shape[left_axis]
    dot = functools.partial(
        lax.dot_general, dimension_numbers=dims, preferred_element_type=jnp.float32
    )
    join = jnp.concatenate
    if 3 * depth <= DEPTH:
        return dot(
            join([left[0], left[1], left[0]], axis=left_axis),
            join([right[0], right[0], right[1]], axis=right_axis),
        )
    if 2 * depth <= DEPTH:
        both = dot(join(left, axis=left_axis), join([right[0], right[0]], axis=right_axis))
        return both + dot(left[0], right[1])
    size = left[0].shape[1 - left_axis]
    both = dot(join(left, axis=1 - left_axis), right[0])
    return both[:size] + (both[size:] + dot(left[0], right[1]))


def square_iota(shape):
    return lax.broadcasted_iota(jnp.int32, shape, 0), lax.broadcasted_iota(jnp.int32, shape, 1)


def pack_kernel(position_ref, compact_hbm, factor_hbm, packed_hbm, compact_ref, factor_ref, packed_ref, in_sems, out_sems):
    blocks, width, band = compact_ref.shape
    half = (width + band) // 2
    row, column = square_iota((width, band))
    upper_part = row + column < half
    frow, fcolumn = square_iota((width, width))

    def fetch(block):
        return (
            pltpu.make_async_copy(compact_hbm.at[0, block], compact_ref.at[block], in_sems.at[0, block]),
            pltpu.make_async_copy(factor_hbm.at[0, block], factor_ref.at[block], in_sems.at[1, block]),
        )

    def deliver(block):
        return pltpu.make_async_copy(packed_ref.at[block], packed_hbm.at[block], out_sems.at[block])

    def scaled(block):
        factor = factor_ref[block]
        diagonal = jnp.where(frow == fcolumn, factor, 0.0)
        down = jnp.sum(diagonal, axis=1, keepdims=True) * 0.5
        across = jnp.sum(diagonal, axis=0, keepdims=True) * 0.5
        inverse = lax.rsqrt(down)
        return compact_ref[block] * (down * inverse), factor * (inverse * lax.rsqrt(across))

    for block in range(blocks):
        for copy in fetch(block):
            copy.start()

    @pl.when(position_ref[0] % 2 == 0)
    def _():
        for block in range(blocks):
            for copy in fetch(block):
                copy.wait()
            packed_ref[block, :, :band] = compact_ref[block]
            packed_ref[block, :, band:] = factor_ref[block]
            deliver(block).start()

    @pl.when(position_ref[0] % 2 == 1)
    def _():
        before = None
        for block in range(blocks):
            for copy in fetch(block):
                copy.wait()
            compact, factor = scaled(block)
            other_compact, other_factor = before or (compact, factor)
            packed_ref[block, :, :band] = jnp.where(upper_part, compact, other_compact)
            packed_ref[block, :, band:] = jnp.where(frow <= fcolumn, factor, other_factor.T)
            deliver(block).start()
            before = compact, factor

    for block in range(blocks):
        deliver(block).wait()


def skew(packed, band):
    _, column = square_iota(packed.shape)
    return pltpu.roll(jnp.where(column < band, packed, 0.0), 0, 1, stride=1, stride_axis=0)


def read_even(packed_ref, flags_ref, window, width):
    band = packed_ref.shape[-1] - width
    packed = packed_ref[window]
    transposed = split(skew(packed, band))
    factor = split(packed[:, band:] * flags_ref[window, :1, :1])
    return transposed, split(product(factor, transposed))


def read_odd(packed_ref, flags_ref, window, width):
    total = packed_ref.shape[-1]
    band = total - width
    half = total // 2
    packed = packed_ref[window]
    skewed = skew(packed, band)
    nothing = jnp.zeros((width, half), jnp.float32)
    above = jnp.concatenate([skewed[:, half:], nothing], axis=1)
    below = jnp.concatenate([nothing, skewed[:, :half]], axis=1)
    mixed = packed[:, band:]
    row, column = square_iota((width, width))
    diagonal = jnp.where(row == column, 2.0, 0.0)
    factor_below = jnp.where(row < column, mixed, diagonal) * flags_ref[window, 0:1, :1]
    factor_above = jnp.where(row < column, mixed.T, diagonal) * flags_ref[window, 1:2, :1]
    odd = flags_ref[window, 2:3, :1] > 0.5
    rows = jnp.concatenate([jnp.where(odd, below, above), jnp.where(odd, above, below)], axis=0)
    square = jnp.zeros((width, width), jnp.float32)
    factor = jnp.concatenate(
        [
            jnp.concatenate([jnp.where(odd, factor_below, factor_above), square], axis=1),
            jnp.concatenate([square, jnp.where(odd, factor_above, factor_below)], axis=1),
        ],
        axis=0,
    )
    return rows, split(factor)


def split_kernel(count, position_ref, first_ref, z_hbm, high_ref, low_ref, flags_ref, z_ref, sem):
    copy = pltpu.make_async_copy(z_hbm.at[:, : z_ref.shape[1]], z_ref, sem)
    copy.start()
    position = position_ref[0]
    row, _ = square_iota(flags_ref.shape[1:])
    for window in range(flags_ref.shape[0]):
        first = first_ref[window]
        if window % 2 == 0:
            flags = jnp.where(position >= first, 1.0, 0.0)
            flags_ref[window] = jnp.full(flags_ref.shape[1:], flags, jnp.float32)
        else:
            below = jnp.where((position < count - 1) & (position >= first), 1.0, 0.0)
            above = jnp.where((position >= 1) & (position - 1 >= first), 1.0, 0.0)
            odd = jnp.where(position % 2 == 1, 1.0, 0.0)
            flags_ref[window] = jnp.where(row == 0, below, jnp.where(row == 1, above, odd))
    copy.wait()
    high_ref[...], low_ref[...] = split(z_ref[...])


def first_kernel(width, flags_ref, packed_ref, high_ref, low_ref, cross_ref, own_ref):
    transposed, scaled = read_even(packed_ref, flags_ref, 0, width)
    rows, _ = read_odd(packed_ref, flags_ref, 1, width)
    partial = product(split(through(rows, transposed, scaled)), (high_ref[...], low_ref[...]))
    cross_ref[...] = partial[:width]
    own_ref[...] = partial[width:]


def through(rows, transposed, scaled):
    return rows - product(split(product(split(rows), transposed, NT)), scaled)


def put(refs, value):
    refs[0][...], refs[1][...] = split(value)


def get(refs):
    return refs[0][...], refs[1][...]


def next_even(packed_ref, flags_ref, window, width):
    transposed, scaled = read_even(packed_ref, flags_ref, window, width)
    rows, _ = read_odd(packed_ref, flags_ref, window + 1, width)
    return transposed, scaled, split(through(rows[:width], transposed, scaled))


def start_kernel(width, order_ref, flags_ref, packed_ref, high_ref, low_ref, z_ref, ahead_ref, mix_ref, *even):
    z_split = get((high_ref, low_ref))
    transposed, scaled = read_even(packed_ref, flags_ref, 0, width)
    z = high_ref[...].astype(jnp.float32) + low_ref[...].astype(jnp.float32)
    z = z - product(transposed, split(product(scaled, z_split)), TN)
    z_ref[...] = z
    transposed, scaled, cross_rows = next_even(packed_ref, flags_ref, 2, width)
    rows, factor = read_odd(packed_ref, flags_ref, 1, width)
    mix_ref[...] = product(cross_rows, split(product(split(rows), factor, TN)))
    ahead_ref[...] = product(cross_rows, split(z))
    for ref, value in zip(even, transposed + scaled + cross_rows):
        ref[...] = value


def message_kernel(width, own, own_in, ahead, mix, message, sum_high, sum_low):
    total = split(own[...] + own_in[...])
    sum_high[...], sum_low[...] = total
    message[:width, :] = ahead[...] - product(split(mix[:, width:]), total)
    message[width:, :] = jnp.zeros((TAIL, message.shape[1]), jnp.float32)
    for group in range(width // TAIL):
        message[width:, group * width : (group + 1) * width] = mix[group * TAIL : (group + 1) * TAIL, :width]


def cross_sum(width, message, message_in, before):
    total = message[:width, :] + message_in[:width, :]
    if before is None:
        return total
    tail = message[width:, :] + message_in[width:, :]
    mix = [tail[:, group * width : (group + 1) * width] for group in range(width // TAIL)]
    return total - product(split(jnp.concatenate(mix, axis=0)), before)


def arrive_kernel(width, first, message, message_in, *refs):
    before = None
    if not first:
        before, refs = get(refs), refs[2:]
    own_sum, refs = get(refs), refs[2:]
    terms, mix_high, mix_low, *out = refs
    cross = split(cross_sum(width, message, message_in, before))
    sums = tuple(jnp.concatenate(pair, axis=0) for pair in zip(cross, own_sum))
    result = terms[...] - product((mix_high[...], mix_low[...]), sums)
    out[0][...], out[1][...] = cross
    out[2][...] = result[:width]
    if len(out) > 3:
        out[3][...] = result[width:]


def state_of(refs, start):
    if start:
        return refs[0][...], refs[1:]
    z, update_high, update_low, cross_high, cross_low, own_high, own_low = refs[:7]
    sums = (
        jnp.concatenate([cross_high[...], own_high[...]], axis=0),
        jnp.concatenate([cross_low[...], own_low[...]], axis=0),
    )
    return z[...] - product((update_high[...], update_low[...]), sums), refs[7:]


def ahead_kernel(width, window, start, more, order_ref, flags_ref, packed_ref, *refs):
    z, refs = state_of(refs, start)
    transposed, scaled, cross_rows = get(refs[0:2]), get(refs[2:4]), get(refs[4:6])
    z_out, terms, mix_high, mix_low, update_high, update_low, *out = refs[6:]
    rows, factor = read_odd(packed_ref, flags_ref, window, width)
    moved = product(split(rows), factor, TN)
    if not start:
        out[0][...] = product(cross_rows, split(moved))
        out = out[1:]
    rows, _ = read_odd(packed_ref, flags_ref, window + 2, width)
    rows = rows[width:]
    if more:
        even = next_even(packed_ref, flags_ref, window + 3, width)
        for ref, value in zip(out, even[0] + even[1] + even[2]):
            ref[...] = value
        rows = jnp.concatenate([rows, even[2][0].astype(jnp.float32) + even[2][1].astype(jnp.float32)], axis=0)
    left = split(through(rows, transposed, scaled))
    left = tuple(jnp.concatenate(pair, axis=0) for pair in zip(scaled, left))
    kept = z.shape[1]
    wide = jnp.concatenate([z, moved], axis=1)
    result = product(left, split(wide))
    terms[...] = result[width:, :kept]
    mix_high[...], mix_low[...] = split(result[width:, kept:])
    wide = wide - product(transposed, split(result[:width]), TN)
    z_out[...] = wide[:, :kept]
    update_high[...], update_low[...] = split(wide[:, kept:])


def end_kernel(width, window, flags_ref, packed_ref, *refs):
    z, refs = state_of(refs, False)
    z_out, update_high, update_low = refs
    z_out[...] = z
    rows, factor = read_odd(packed_ref, flags_ref, window, width)
    update_high[...], update_low[...] = split(product(split(rows), factor, TN))


def last_kernel(width, live_ref, message, message_in, before_high, before_low, own, own_in, z_ref, update_high, update_low, out_hbm, out_ref, sems):
    rows, kept = z_ref.shape
    total = out_ref.shape[1]
    pieces = PIECES
    size = kept // pieces

    def deliver(piece):
        begin, end = piece * size, (piece + 1) * size if piece < pieces else total
        return pltpu.make_async_copy(
            out_ref.at[:, begin:end], out_hbm.at[:, begin:end], sems.at[piece]
        )

    out_ref[:, kept:] = jnp.zeros((rows, total - kept), jnp.float32)
    deliver(pieces).start()
    cross = cross_sum(width, message, message_in, (before_high[...], before_low[...]))
    for piece in range(pieces):
        here = slice(piece * size, (piece + 1) * size)
        sums = jnp.concatenate([cross[:, here], own[:, here] + own_in[:, here]], axis=0)
        z = z_ref[:, here] - product((update_high[...], update_low[...]), split(sums))
        _, column = square_iota(z.shape)
        out_ref[:, here] = jnp.where(column + piece * size < live_ref[0], z, 0.0)
        deliver(piece).start()
    for piece in range(pieces + 1):
        deliver(piece).wait()


def call(kernel, outs, ins, *operands, flops=0, scratch=(), out_specs=None, limit=40 << 20):
    shapes = [jax.ShapeDtypeStruct(shape, dtype) for shape, dtype in outs]
    return pl.pallas_call(
        kernel,
        out_shape=shapes,
        in_specs=ins,
        out_specs=out_specs or [VMEM] * len(shapes),
        scratch_shapes=scratch,
        cost_estimate=pl.CostEstimate(flops=flops, bytes_accessed=1 << 20, transcendentals=0),
        compiler_params=pltpu.CompilerParams(vmem_limit_bytes=limit),
    )(*operands)


def body(eigvecs, reflectors, factors, first_block, live_count):
    count = lax.axis_size("row")
    position = lax.axis_index("row").astype(jnp.int32).reshape(1)
    row_count, col_count = eigvecs.shape
    share, blocks, width, band = reflectors.shape
    block_rows = width + band
    assert row_count == block_rows and share == 1 and blocks == count
    windows = share * count
    kept = 3 * col_count // 4
    f32, bf16 = jnp.float32, jnp.bfloat16

    packed = call(
        pack_kernel,
        [((blocks, width, block_rows), f32)],
        [SMEM, HBM, HBM],
        position,
        reflectors,
        factors,
        out_specs=[HBM],
        limit=None,
        scratch=[
            pltpu.VMEM((blocks, width, band), f32),
            pltpu.VMEM((blocks, width, width), f32),
            pltpu.VMEM((blocks, width, block_rows), f32),
            pltpu.SemaphoreType.DMA((2, blocks)),
            pltpu.SemaphoreType.DMA((blocks,)),
        ],
    )[0]
    packed = lax.all_to_all(packed, "row", split_axis=0, concat_axis=0, tiled=True)
    high, low, flags = call(
        functools.partial(split_kernel, count),
        [((row_count, kept), bf16)] * 2 + [((windows, 8, 128), f32)],
        [SMEM, SMEM, HBM],
        position,
        first_block,
        eigvecs,
        scratch=[pltpu.VMEM((row_count, kept), f32), pltpu.SemaphoreType.DMA],
    )

    def swap(x, start):
        pairs = [(i, i + 1) for i in range(start, count - 1, 2)]
        return lax.ppermute(x, "row", pairs + [(j, i) for i, j in pairs])

    small = ((width, kept), f32)
    half_sum = [((width, kept), bf16)] * 2
    even = [((width, block_rows), bf16)] * 6
    update = [((block_rows, 2 * width), bf16)] * 2
    rounds = windows // 2
    message, own = call(
        functools.partial(first_kernel, width),
        [small, small],
        [VMEM] * 4,
        flags,
        packed,
        high,
        low,
    )
    message_in, own_in = swap(message, 1), swap(own, 0)
    z, ahead, mix, *even_arrays = call(
        functools.partial(start_kernel, width),
        [((row_count, kept), f32), small, ((width, 2 * width), f32)] + even,
        [ANY] + [VMEM] * 4,
        message,
        flags,
        packed,
        high,
        low,
        flops=10**9,
    )
    state = (z,)
    before = ()
    for number in range(1, rounds):
        window = 2 * number - 1
        more = number < rounds - 1

        def look_ahead(order):
            terms = (2 if more else 1) * width
            outs = [((row_count, kept), f32), ((terms, kept), f32)]
            outs += [((terms, 2 * width), bf16)] * 2 + update
            outs += [((width, 2 * width), f32)] if number > 1 else []
            outs += even if more else []
            operands = (order, flags, packed, *state, *even_arrays)
            return call(
                functools.partial(ahead_kernel, width, window, number == 1, more),
                outs,
                [ANY] + [VMEM] * (len(operands) - 1),
                *operands,
                flops=10**9,
            )

        if number > 1:
            z, terms, mix_high, mix_low, update_high, update_low, mix, *even_arrays = look_ahead(own)
        next_message, *own_sum = call(
            functools.partial(message_kernel, width),
            [((width + TAIL, kept), f32)] + half_sum,
            [VMEM] * 4,
            own,
            own_in,
            ahead,
            mix,
        )
        next_in = swap(next_message, 1)
        if number == 1:
            z, terms, mix_high, mix_low, update_high, update_low, *even_arrays = look_ahead(next_message)
        operands = (message, message_in, *before, *own_sum, terms, mix_high, mix_low)
        cross_high, cross_low, own, *ahead = call(
            functools.partial(arrive_kernel, width, number == 1),
            half_sum + [small] * (2 if more else 1),
            [VMEM] * len(operands),
            *operands,
        )
        ahead = ahead[0] if more else None
        before = (cross_high, cross_low)
        own_in = swap(own, 0)
        state = (z, update_high, update_low, cross_high, cross_low, *own_sum)
        message, message_in = next_message, next_in
    z, update_high, update_low = call(
        functools.partial(end_kernel, width, windows - 1),
        [((row_count, kept), f32)] + update,
        [VMEM] * (2 + len(state)),
        flags,
        packed,
        *state,
        flops=10**9,
    )
    return call(
        functools.partial(last_kernel, width),
        [((row_count, col_count), f32)],
        [SMEM] + [VMEM] * 9,
        live_count,
        message,
        message_in,
        *before,
        own,
        own_in,
        z,
        update_high,
        update_low,
        out_specs=[HBM],
        scratch=[pltpu.VMEM((row_count, col_count), f32), pltpu.SemaphoreType.DMA((PIECES + 1,))],
    )[0]


def solution(mesh):
    placed = (
        P("row", "col"),
        P("row", None, None, None),
        P("row", None, None, None),
        P(),
        P("col"),
    )
    return jax.shard_map(
        body, mesh=mesh, in_specs=placed, out_specs=P("row", "col"), check_vma=False
    )
```

```python
import functools

import jax
import jax.numpy as jnp
from jax import lax
from jax.experimental import pallas as pl
from jax.experimental.pallas import tpu as pltpu
from jax.sharding import PartitionSpec as P

VMEM = pl.BlockSpec(memory_space=pltpu.VMEM)
SMEM = pl.BlockSpec(memory_space=pltpu.SMEM)
NN = (((1,), (0,)), ((), ()))
NT = (((1,), (1,)), ((), ()))
TN = (((0,), (0,)), ((), ()))
ANY = pl.BlockSpec(memory_space=pl.ANY)
HBM = pl.BlockSpec(memory_space=pltpu.HBM)
PIECES = 3
DEPTH = 256
TAIL = 8


def split(x):
    high = x.astype(jnp.bfloat16)
    return high, (x - high.astype(jnp.float32)).astype(jnp.bfloat16)


def product(left, right, dims=NN):
    ((left_axis,), (right_axis,)), _ = dims
    depth = left[0].shape[left_axis]
    dot = functools.partial(
        lax.dot_general, dimension_numbers=dims, preferred_element_type=jnp.float32
    )
    join = jnp.concatenate
    if 3 * depth <= DEPTH:
        return dot(
            join([left[0], left[1], left[0]], axis=left_axis),
            join([right[0], right[0], right[1]], axis=right_axis),
        )
    if 2 * depth <= DEPTH:
        both = dot(join(left, axis=left_axis), join([right[0], right[0]], axis=right_axis))
        return both + dot(left[0], right[1])
    size = left[0].shape[1 - left_axis]
    both = dot(join(left, axis=1 - left_axis), right[0])
    return both[:size] + (both[size:] + dot(left[0], right[1]))


def square_iota(shape):
    return lax.broadcasted_iota(jnp.int32, shape, 0), lax.broadcasted_iota(jnp.int32, shape, 1)


def pack_kernel(position_ref, compact_hbm, factor_hbm, packed_hbm, compact_ref, factor_ref, packed_ref, in_sems, out_sems):
    blocks, width, band = compact_ref.shape
    half = (width + band) // 2
    row, column = square_iota((width, band))
    upper_part = row + column < half
    frow, fcolumn = square_iota((width, width))

    def fetch(block):
        return (
            pltpu.make_async_copy(compact_hbm.at[0, block], compact_ref.at[block], in_sems.at[0, block]),
            pltpu.make_async_copy(factor_hbm.at[0, block], factor_ref.at[block], in_sems.at[1, block]),
        )

    def deliver(block):
        return pltpu.make_async_copy(packed_ref.at[block], packed_hbm.at[block], out_sems.at[block])

    for block in range(blocks):
        for copy in fetch(block):
            copy.start()

    for block in range(blocks):
        for copy in fetch(block):
            copy.wait()

    @pl.when(position_ref[0] % 2 == 0)
    def _():
        for block in range(blocks):
            packed_ref[block, :, :band] = compact_ref[block]
            packed_ref[block, :, band:] = factor_ref[block]
            deliver(block).start()

    @pl.when(position_ref[0] % 2 == 1)
    def _():
        on_diagonal = frow == fcolumn
        halves = [
            0.5 * jnp.sum(jnp.where(on_diagonal, factor_ref[block], 0.0), axis=0, keepdims=True)
            for block in range(blocks)
        ]
        halves = jnp.concatenate(halves, axis=0)
        inverse = lax.rsqrt(halves)
        scales, inverses = (halves * inverse).T, inverse.T
        before = None
        for block in range(blocks):
            compact = compact_ref[block] * scales[:, block : block + 1]
            factor = factor_ref[block] * (inverses[:, block : block + 1] * inverse[block : block + 1, :])
            other_compact, other_factor = before or (compact, factor)
            packed_ref[block, :, :band] = jnp.where(upper_part, compact, other_compact)
            packed_ref[block, :, band:] = jnp.where(frow <= fcolumn, factor, other_factor.T)
            deliver(block).start()
            before = compact, factor

    for block in range(blocks):
        deliver(block).wait()


def skew(packed, band):
    _, column = square_iota(packed.shape)
    return pltpu.roll(jnp.where(column < band, packed, 0.0), 0, 1, stride=1, stride_axis=0)


def read_even(packed_ref, flags_ref, window, width):
    band = packed_ref.shape[-1] - width
    packed = packed_ref[window]
    transposed = split(skew(packed, band))
    factor = split(packed[:, band:] * flags_ref[window, :1, :1])
    return transposed, split(product(factor, transposed))


def read_odd(packed_ref, flags_ref, window, width):
    total = packed_ref.shape[-1]
    band = total - width
    half = total // 2
    packed = packed_ref[window]
    skewed = skew(packed, band)
    nothing = jnp.zeros((width, half), jnp.float32)
    above = jnp.concatenate([skewed[:, half:], nothing], axis=1)
    below = jnp.concatenate([nothing, skewed[:, :half]], axis=1)
    mixed = packed[:, band:]
    row, column = square_iota((width, width))
    diagonal = jnp.where(row == column, 2.0, 0.0)
    factor_below = jnp.where(row < column, mixed, diagonal) * flags_ref[window, 0:1, :1]
    factor_above = jnp.where(row < column, mixed.T, diagonal) * flags_ref[window, 1:2, :1]
    odd = flags_ref[window, 2:3, :1] > 0.5
    rows = jnp.concatenate([jnp.where(odd, below, above), jnp.where(odd, above, below)], axis=0)
    square = jnp.zeros((width, width), jnp.float32)
    factor = jnp.concatenate(
        [
            jnp.concatenate([jnp.where(odd, factor_below, factor_above), square], axis=1),
            jnp.concatenate([square, jnp.where(odd, factor_above, factor_below)], axis=1),
        ],
        axis=0,
    )
    return rows, split(factor)


def split_kernel(count, position_ref, first_ref, z_hbm, high_ref, low_ref, flags_ref, z_ref, sem):
    copy = pltpu.make_async_copy(z_hbm.at[:, : z_ref.shape[1]], z_ref, sem)
    copy.start()
    position = position_ref[0]
    row, _ = square_iota(flags_ref.shape[1:])
    for window in range(flags_ref.shape[0]):
        first = first_ref[window]
        if window % 2 == 0:
            flags = jnp.where(position >= first, 1.0, 0.0)
            flags_ref[window] = jnp.full(flags_ref.shape[1:], flags, jnp.float32)
        else:
            below = jnp.where((position < count - 1) & (position >= first), 1.0, 0.0)
            above = jnp.where((position >= 1) & (position - 1 >= first), 1.0, 0.0)
            odd = jnp.where(position % 2 == 1, 1.0, 0.0)
            flags_ref[window] = jnp.where(row == 0, below, jnp.where(row == 1, above, odd))
    copy.wait()
    high_ref[...], low_ref[...] = split(z_ref[...])


def first_kernel(width, flags_ref, packed_ref, high_ref, low_ref, cross_ref, own_ref):
    transposed, scaled = read_even(packed_ref, flags_ref, 0, width)
    rows, _ = read_odd(packed_ref, flags_ref, 1, width)
    partial = product(split(through(rows, transposed, scaled)), (high_ref[...], low_ref[...]))
    cross_ref[...] = partial[:width]
    own_ref[...] = partial[width:]


def through(rows, transposed, scaled):
    return rows - product(split(product(split(rows), transposed, NT)), scaled)


def put(refs, value):
    refs[0][...], refs[1][...] = split(value)


def store(refs, values):
    for ref, value in zip(refs, values):
        ref[...] = value


def load(refs):
    return tuple(ref[...] for ref in refs)


def join(*parts, axis=0):
    return tuple(jnp.concatenate(pair, axis=axis) for pair in zip(*parts))


def apply_even(z, transposed, scaled):
    return z - product(transposed, split(product(scaled, split(z))), TN)


def spread(packed_ref, flags_ref, window, width):
    rows, factor = read_odd(packed_ref, flags_ref, window, width)
    return split(product(split(rows), factor, TN))


def next_even(packed_ref, flags_ref, window, width):
    transposed, scaled = read_even(packed_ref, flags_ref, window, width)
    rows, _ = read_odd(packed_ref, flags_ref, window + 1, width)
    return transposed, scaled, split(through(rows[:width], transposed, scaled))


def start_kernel(width, order_ref, flags_ref, packed_ref, high_ref, low_ref, z_ref, ahead_ref, mix_ref, mix_next_ref, *out):
    transposed, scaled, cross_rows = next_even(packed_ref, flags_ref, 2, width)
    first = spread(packed_ref, flags_ref, 1, width)
    mix_ref[...] = product(cross_rows, first)
    z_split = load((high_ref, low_ref))
    even = read_even(packed_ref, flags_ref, 0, width)
    z = high_ref[...].astype(jnp.float32) + low_ref[...].astype(jnp.float32)
    z = z - product(even[0], split(product(even[1], z_split)), TN)
    z_ref[...] = z
    ahead_ref[...] = product(cross_rows, split(z))
    following = next_even(packed_ref, flags_ref, 4, width)
    second = spread(packed_ref, flags_ref, 3, width)
    mix_next_ref[...] = product(following[2], second)
    store(out, transposed + scaled + following[0] + following[1] + following[2] + first + second)


def message_kernel(width, tails, own, own_in, ahead, mix, *refs):
    squares = (mix,) + refs[: max(tails - 1, 0)] if tails != 1 else refs[:1]
    message, sum_high, sum_low = refs[-3:]
    total = split(own[...] + own_in[...])
    sum_high[...], sum_low[...] = total
    message[:width, :] = ahead[...] - product(split(mix[:, width:]), total)
    for number in range(tails):
        top = width + number * TAIL
        message[top : top + TAIL, :] = jnp.zeros((TAIL, message.shape[1]), jnp.float32)
        for group in range(width // TAIL):
            message[top : top + TAIL, group * width : (group + 1) * width] = squares[number][
                group * TAIL : (group + 1) * TAIL, :width
            ]


def square_sum(width, number, message, message_in):
    top = width + number * TAIL
    tail = message[top : top + TAIL, :] + message_in[top : top + TAIL, :]
    parts = [tail[:, group * width : (group + 1) * width] for group in range(width // TAIL)]
    return split(jnp.concatenate(parts, axis=0))


def arrive_kernel(width, kind, sends, more, message, message_in, *refs):
    cross = message[:width, :] + message_in[:width, :]
    if kind == 2:
        cross = cross - product(square_sum(width, 0, message, message_in), load(refs[:2]))
        refs = refs[2:]
    if kind == 3:
        cross = cross - refs[0][...]
        refs = refs[1:]
    cross = split(cross)
    own_sum, terms, mix, out = load(refs[:2]), refs[2], load(refs[3:5]), refs[5:]
    result = terms[...] - product(mix, join(cross, own_sum))
    store(out[:2], cross)
    out[2][...] = result[:width]
    out = out[3:]
    if more:
        out[0][...] = result[width:]
        out = out[1:]
    if sends:
        store(out, square_sum(width, 1 if kind == 2 else 0, message, message_in))


def ahead_kernel(width, number, rounds, order_ref, flags_ref, packed_ref, *refs):
    window = 2 * number - 1
    carry = number < rounds - 2
    if number == 1:
        z, refs = refs[0][...], refs[1:]
    else:
        z, update, sums = refs[0][...], load(refs[1:3]), join(load(refs[3:5]), load(refs[5:7]))
        z, refs = z - product(update, sums), refs[7:]
    if number > 2:
        refs[-1][...] = product(load(refs[2:4]), load(refs[0:2]))
        refs = refs[4:-1]
    transposed, scaled, cross_rows, moved = (load(refs[at : at + 2]) for at in range(0, 8, 2))
    z_out, terms, mix_high, mix_low, *out = refs[8:]
    rows, _ = read_odd(packed_ref, flags_ref, window + 2, width)
    left = join(split(rows[width:]), cross_rows)
    left = split(through(rows_of(left), transposed, scaled))
    if carry:
        left = join(scaled, left)
    kept = z.shape[1]
    z_split = split(z)
    result = product(left, join(z_split, moved, axis=1))
    skip = width if carry else 0
    terms[...] = result[skip:, :kept]
    mix_high[...], mix_low[...] = split(result[skip:, kept:])
    if number > 1:
        following = spread(packed_ref, flags_ref, window + 2, width)
        out[0][...] = product(cross_rows, following)
        store(out[1:3], following)
        out = out[3:]
    if carry:
        inner = split(result[:width])
        moved = moved[0].astype(jnp.float32) + moved[1].astype(jnp.float32)
        z_out[...] = z - product(transposed, tuple(part[:, :kept] for part in inner), TN)
        put(out[:2], moved - product(transposed, tuple(part[:, kept:] for part in inner), TN))
        even = next_even(packed_ref, flags_ref, window + 5, width)
        store(out[2:], even[0] + even[1] + even[2])
    else:
        z_out[...] = z


def rows_of(parts):
    return parts[0].astype(jnp.float32) + parts[1].astype(jnp.float32)


def ahead_last_kernel(width, rounds, order_ref, flags_ref, packed_ref, z_ref, *refs):
    moved, cross, own_sum, transposed, scaled, transposed_next, scaled_next, moved_next = (
        load(refs[at : at + 2]) for at in range(0, 16, 2)
    )
    refs = refs[16:]
    if rounds > 3:
        refs[-1][...] = product(load(refs[:2]), cross)
        refs = refs[2:-1]
    terms, mix_high, mix_low = refs
    rows, _ = read_odd(packed_ref, flags_ref, 2 * rounds - 1, width)
    left = through(rows[width:], transposed_next, scaled_next)
    mix_high[...], mix_low[...] = split(product(split(left), moved_next))
    left = split(through(left, transposed, scaled))
    effect = split(product(left, moved))
    terms[...] = product(left, split(z_ref[...])) - product(effect, join(cross, own_sum))


def end_kernel(width, rounds, flags_ref, packed_ref, z_ref, *refs):
    z, pairs = z_ref[...], [load(refs[at : at + 2]) for at in range(0, 20, 2)]
    moved, cross, own_sum, transposed, scaled = pairs[:5]
    z = apply_even(z - product(moved, join(cross, own_sum)), transposed, scaled)
    moved, cross, own_sum, transposed, scaled = pairs[5:]
    z = apply_even(z - product(moved, join(cross, own_sum)), transposed, scaled)
    z_out, update_high, update_low = refs[20:]
    z_out[...] = z
    store((update_high, update_low), spread(packed_ref, flags_ref, 2 * rounds - 1, width))


def near_kernel(width, z_ref, update_high, update_low, message, square_high, square_low, before_high, before_low, own, own_in, z_out):
    cross = message[...] - product(load((square_high, square_low)), load((before_high, before_low)))
    sums = join(split(cross), split(own[...] + own_in[...]))
    z_out[...] = z_ref[...] - product(load((update_high, update_low)), sums)


def last_kernel(width, live_ref, message_in, z_ref, update_high, update_low, out_hbm, out_ref, sems):
    rows, kept = z_ref.shape
    total = out_ref.shape[1]
    pieces = PIECES
    size = kept // pieces

    def deliver(piece):
        begin, end = piece * size, (piece + 1) * size if piece < pieces else total
        return pltpu.make_async_copy(
            out_ref.at[:, begin:end], out_hbm.at[:, begin:end], sems.at[piece]
        )

    out_ref[:, kept:] = jnp.zeros((rows, total - kept), jnp.float32)
    deliver(pieces).start()
    update = update_high[:, :width], update_low[:, :width]
    for piece in range(pieces):
        here = slice(piece * size, (piece + 1) * size)
        z = z_ref[:, here] - product(update, split(message_in[:, here]))
        _, column = square_iota(z.shape)
        out_ref[:, here] = jnp.where(column + piece * size < live_ref[0], z, 0.0)
        deliver(piece).start()
    for piece in range(pieces + 1):
        deliver(piece).wait()


def call(kernel, outs, ins, *operands, flops=0, scratch=(), out_specs=None, limit=40 << 20):
    shapes = [jax.ShapeDtypeStruct(shape, dtype) for shape, dtype in outs]
    return pl.pallas_call(
        kernel,
        out_shape=shapes,
        in_specs=ins,
        out_specs=out_specs or [VMEM] * len(shapes),
        scratch_shapes=scratch,
        cost_estimate=pl.CostEstimate(flops=flops, bytes_accessed=1 << 20, transcendentals=0),
        compiler_params=pltpu.CompilerParams(vmem_limit_bytes=limit),
    )(*operands)


def body(eigvecs, reflectors, factors, first_block, live_count):
    count = lax.axis_size("row")
    position = lax.axis_index("row").astype(jnp.int32).reshape(1)
    row_count, col_count = eigvecs.shape
    share, blocks, width, band = reflectors.shape
    block_rows = width + band
    assert row_count == block_rows and share == 1 and blocks == count
    windows = share * count
    kept = 3 * col_count // 4
    f32, bf16 = jnp.float32, jnp.bfloat16

    packed = call(
        pack_kernel,
        [((blocks, width, block_rows), f32)],
        [SMEM, HBM, HBM],
        position,
        reflectors,
        factors,
        out_specs=[HBM],
        limit=None,
        scratch=[
            pltpu.VMEM((blocks, width, band), f32),
            pltpu.VMEM((blocks, width, width), f32),
            pltpu.VMEM((blocks, width, block_rows), f32),
            pltpu.SemaphoreType.DMA((2, blocks)),
            pltpu.SemaphoreType.DMA((blocks,)),
        ],
    )[0]
    packed = lax.all_to_all(packed, "row", split_axis=0, concat_axis=0, tiled=True)
    high, low, flags = call(
        functools.partial(split_kernel, count),
        [((row_count, kept), bf16)] * 2 + [((windows, 8, 128), f32)],
        [SMEM, SMEM, HBM],
        position,
        first_block,
        eigvecs,
        scratch=[pltpu.VMEM((row_count, kept), f32), pltpu.SemaphoreType.DMA],
    )

    def swap(x, start):
        pairs = [(i, i + 1) for i in range(start, count - 1, 2)]
        return lax.ppermute(x, "row", pairs + [(j, i) for i, j in pairs])

    small = ((width, kept), f32)
    state_shape = ((row_count, kept), f32)
    square = ((width, 2 * width), f32)
    half_sum = [((width, kept), bf16)] * 2
    half_square = [((width, width), bf16)] * 2
    even_shape = [((width, block_rows), bf16)] * 4
    rows_shape = [((width, block_rows), bf16)] * 2
    update = [((block_rows, 2 * width), bf16)] * 2
    rounds = windows // 2
    assert rounds >= 4

    def kernel_call(kernel, outs, *operands, order=None, flops=10**9):
        ins = [VMEM] * len(operands)
        if order is not None:
            ins, operands = [ANY] + ins, (order,) + operands
        return call(kernel, outs, ins, *operands, flops=flops)

    message, own = kernel_call(
        functools.partial(first_kernel, width), [small, small], flags, packed, high, low
    )
    message_in, own_in = swap(message, 1), swap(own, 0)
    z, ahead, mix, mix_next, *rest = kernel_call(
        functools.partial(start_kernel, width),
        [state_shape, small, square, square] + even_shape * 2 + rows_shape + update * 2,
        flags,
        packed,
        high,
        low,
        order=message,
    )
    even = {2: rest[0:4], 4: rest[4:8]}
    cross_rows = rest[8:10]
    moved = {1: rest[10:12], 2: rest[12:14]}
    sums = {}
    state = (z,)
    squares = effect = ()
    for number in range(1, rounds):

        def look_ahead(order):
            late = number == rounds - 1
            carry = number < rounds - 2
            terms = ((1 if late else 2) * width, kept), f32
            mixes = [((terms[0][0], 2 * width), bf16)] * 2
            extra = [small] if number > 2 else []
            if late:
                return kernel_call(
                    functools.partial(ahead_last_kernel, width, rounds),
                    [terms] + mixes + extra,
                    flags,
                    packed,
                    z,
                    *moved[number - 1],
                    *sums[number - 1],
                    *even[2 * number - 2],
                    *even[2 * number],
                    *moved[number],
                    *squares,
                    order=order,
                )
            return kernel_call(
                functools.partial(ahead_kernel, width, number, rounds),
                [state_shape, terms]
                + mixes
                + ([square] + update if number > 1 else [])
                + (update + even_shape + rows_shape if carry else [])
                + extra,
                flags,
                packed,
                *state,
                *((*sums[number - 1][:2], *squares) if number > 2 else ()),
                *even[2 * number],
                *cross_rows,
                *moved[number],
                order=order,
            )

        def unpack(results):
            results = list(results)
            found = {}
            if number > 2:
                found["effect"] = (results.pop(),)
            if number < rounds - 1:
                found["z"] = results.pop(0)
            found["terms"], found["mixes"] = results[0], results[1:3]
            results = results[3:]
            if 1 < number < rounds - 1:
                found["mix_next"] = results[0]
                moved[number + 1] = results[1:3]
                results = results[3:]
            if number < rounds - 2:
                found["update"] = results[0:2]
                even[2 * number + 4] = results[2:6]
                found["cross_rows"] = results[6:8]
            return found

        found = unpack(look_ahead(own)) if number > 1 else None
        if number > 1 and number < rounds - 1:
            mix_next = found["mix_next"]
        tails = 2 if number == 1 else 1 if number < rounds - 1 else 0
        next_message, *own_sum = kernel_call(
            functools.partial(message_kernel, width, tails),
            [((width + tails * TAIL, kept), f32)] + half_sum,
            own,
            own_in,
            ahead,
            mix,
            *((mix_next,) if tails else ()),
            flops=0,
        )
        next_in = swap(next_message, 1)
        if number == 1:
            found = unpack(look_ahead(next_message))
        kind = min(number, 3)
        more = number < rounds - 1
        sends = 1 < number
        taken = (*sums[number - 1][:2],) if kind == 2 else found.get("effect", ())
        cross_high, cross_low, own, *rest = kernel_call(
            functools.partial(arrive_kernel, width, kind, sends, more),
            half_sum + [small] * (2 if more else 1) + (half_square if sends else []),
            message,
            message_in,
            *taken,
            *own_sum,
            found["terms"],
            *found["mixes"],
            flops=0,
        )
        if more:
            ahead, rest = rest[0], rest[1:]
        squares = tuple(rest)
        own_in = swap(own, 0)
        sums[number] = (cross_high, cross_low, *own_sum)
        z = found.get("z", z)
        if "update" in found:
            state = (z, *found["update"], *sums[number])
            cross_rows = found["cross_rows"]
        mix = mix_next
        message, message_in = next_message, next_in
    z, *spread_last = kernel_call(
        functools.partial(end_kernel, width, rounds),
        [state_shape] + update,
        flags,
        packed,
        z,
        *moved[rounds - 2],
        *sums[rounds - 2],
        *even[windows - 4],
        *moved[rounds - 1],
        *sums[rounds - 1],
        *even[windows - 2],
    )
    z = kernel_call(
        functools.partial(near_kernel, width),
        [state_shape],
        z,
        *spread_last,
        message,
        *squares,
        *sums[rounds - 1][:2],
        own,
        own_in,
    )[0]
    return call(
        functools.partial(last_kernel, width),
        [((row_count, col_count), f32)],
        [SMEM] + [VMEM] * 4,
        live_count,
        message_in,
        z,
        *spread_last,
        out_specs=[HBM],
        scratch=[pltpu.VMEM((row_count, col_count), f32), pltpu.SemaphoreType.DMA((PIECES + 1,))],
    )[0]


def solution(mesh):
    placed = (
        P("row", "col"),
        P("row", None, None, None),
        P("row", None, None, None),
        P(),
        P("col"),
    )
    return jax.shard_map(
        body, mesh=mesh, in_specs=placed, out_specs=P("row", "col"), check_vma=False
    )
```
